32 devices in a mesh: clips: 2 (over y), tm: 4 (over z), rows: 2 (over x), cols: 2 (over core).
Axes of the slice: x: 2, y: 2, z: 4, core: 2. Of those that a mesh axis runs over, the one named last changes fastest.
Arguments:
- latent: bfloat16 [16, 4, 64, 384], P(('clips', 'tm'), 'rows', 'cols'), parts along dimension 0, may hold values from -400 to 400, as said below
- norm_gain: float32 [384], replicated, may hold values from 0.1 to 1.9
- time_weight: bfloat16 [3, 384, 768], replicated, may hold values from -0.1875 to 0.1875
- time_bias: float32 [768], replicated, may hold values from -3 to 3
- space_weight: bfloat16 [3, 3, 384, 192], replicated, may hold values from -0.109375 to 0.109375
- space_bias: float32 [192], replicated, may hold values from -3 to 3
Outputs:
- decoded: bfloat16 [32, 8, 128, 192], P(('clips', 'tm'), 'rows', 'cols'), parts along dimension 0
The draws below stay inside these ranges and needn't reach their ends.
There are 2 independent parts, one for each index of `clips`. The reference program is written for one: setup_inputs(seed, part) draws one part's arguments, and reference() takes and returns one part's arrays. A program takes and returns all parts, laid end to end along the dimension named above; an argument that names none is the same for every part. Nothing has to cross between parts.
Inputs may be any that keep to these rules, and one draw needn't show every extreme that they name: `latent`: real-valued activations.
All inputs are finite; a program needn't handle non-finite values.
Results may differ from the reference program's by a relative error of at most 0.0051.
Values may be sent and summed in bfloat16 or wider, within the bound.
A program may use at most 64 MiB of HBM per device.

```python
import math
import jax
import jax.numpy as jnp
from jax import lax

C = 384
C_OUT = 192
FRAMES = 8
HEIGHT = 4
WIDTH = 64


def draw_latent(key, part):
    base_key, chan_key, voxel_key = jax.random.split(key, 3)
    shape = (FRAMES, HEIGHT, WIDTH, C)
    chan_scale = jnp.exp(jax.random.uniform(chan_key, (C,), jnp.float32, 0.0, math.log(10.0)))
    voxel_scale = jnp.exp(jax.random.uniform(voxel_key, (FRAMES, HEIGHT, WIDTH, 1), jnp.float32, 0.0, math.log(10.0)))
    base = jnp.clip(jax.random.normal(base_key, shape, jnp.float32), -4.0, 4.0)
    return (base * chan_scale * voxel_scale).astype(jnp.bfloat16)


def noise(key, dims, width, bound, held_as=jnp.bfloat16):
    values = width * jax.random.normal(key, dims, jnp.float32)
    return jnp.clip(values, min=-bound, max=bound).astype(held_as)


def setup_inputs(seed: int = 0, part: int = 0) -> dict:
    key_list = jax.random.split(jax.random.key(seed), 7)
    part_splits = jax.random.split(jax.random.fold_in(key_list[6], part), 7)
    latent = draw_latent(jax.random.fold_in(jax.random.fold_in(key_list[6], part), 71), part)
    norm_gain = jnp.clip(1.0 + 0.18 * jax.random.normal(key_list[1], (C,), jnp.float32), 0.1, 1.9)
    time_weight = noise(key_list[2], (3, C, 2 * C), (3 * C) ** -0.5, 0.1875)
    time_bias = noise(key_list[3], (2 * C,), 0.5, 3.0, jnp.float32)
    space_weight = noise(key_list[4], (3, 3, C, C_OUT), (9 * C) ** -0.5, 0.109375)
    space_bias = noise(key_list[5], (C_OUT,), 0.5, 3.0, jnp.float32)
    return dict(latent=latent, norm_gain=norm_gain, time_weight=time_weight, time_bias=time_bias, space_weight=space_weight, space_bias=space_bias)


def pre_activate(latent, norm_gain):
    values = latent.astype(jnp.float32)
    mean_square = lax.optimization_barrier(jnp.mean(values * values, axis=-1, keepdims=True))
    scaled = values * lax.rsqrt(mean_square + 1e-06) * norm_gain.astype(jnp.float32)
    return jax.nn.silu(scaled).astype(jnp.bfloat16)

def time_conv(extended, time_weight, time_bias):
    frames = extended.shape[0] - 2
    height_in = extended.shape[1]
    width_in = extended.shape[2]
    channels = extended.shape[3]
    summed = jnp.zeros((frames * height_in * width_in, time_weight.shape[2]), jnp.float32)
    for offset in range(3):
        window = extended[offset:offset + frames].reshape(-1, channels)
        summed = summed + jnp.dot(window, time_weight[offset], preferred_element_type=jnp.float32)
    summed = summed + time_bias.astype(jnp.float32)
    return summed.astype(jnp.bfloat16).reshape(frames, height_in, width_in, time_weight.shape[2])

def split_frames(stacked):
    frames, height_in, width_in, doubled = stacked.shape
    channels = doubled // 2
    parted = stacked.reshape(frames, height_in, width_in, 2, channels)
    return jnp.moveaxis(parted, 3, 1).reshape(2 * frames, height_in, width_in, channels)

def space_conv(margined, space_weight, space_bias):
    enlarged = jnp.repeat(jnp.repeat(margined, 2, axis=1), 2, axis=2)[:, 1:-1, 1:-1]
    frames = enlarged.shape[0]
    out_rows = enlarged.shape[1] - 2
    out_cols = enlarged.shape[2] - 2
    channels = enlarged.shape[3]
    summed = jnp.zeros((frames * out_rows * out_cols, space_weight.shape[3]), jnp.float32)
    for row_tap in range(3):
        patches = jnp.concatenate([enlarged[:, row_tap:row_tap + out_rows, col_tap:col_tap + out_cols] for col_tap in range(3)], axis=-1)
        summed = summed + jnp.dot(patches.reshape(-1, 3 * channels), space_weight[row_tap].reshape(3 * channels, -1), preferred_element_type=jnp.float32)
    summed = summed + space_bias.astype(jnp.float32)
    return summed.astype(jnp.bfloat16).reshape(frames, out_rows, out_cols, space_weight.shape[3])

def reference(latent, norm_gain, time_weight, time_bias, space_weight, space_bias):
    activated = pre_activate(latent, norm_gain)
    zero_frames = jnp.zeros((2,) + activated.shape[1:], activated.dtype)
    extended = jnp.concatenate([zero_frames, activated], axis=0)
    stacked = time_conv(extended, time_weight, time_bias)
    frames = split_frames(stacked)
    margined = jnp.pad(frames, ((0, 0), (1, 1), (1, 1), (0, 0)))

    def one_frame(single):
        return space_conv(single[None], space_weight, space_bias)[0]
    return lax.map(one_frame, margined)
```

```python
import functools

import jax
import jax.numpy as jnp
from jax import lax
from jax.experimental import pallas as pl
from jax.experimental.pallas import tpu as pltpu
from jax.sharding import PartitionSpec as P

F32 = jnp.float32
BF16 = jnp.bfloat16
MESH = pl.DeviceIdType.MESH
KINDS = [(dt, dr, dc) for dt in (1, 0) for dr in (0, -1, 1) for dc in (0, 1) if (dt, dr, dc) != (0, 0, 0)]


def activate(raw, gain):
    values = raw.astype(F32)
    mean_square = jnp.mean(values * values, axis=-1, keepdims=True)
    scaled = values * lax.rsqrt(mean_square + 1e-06) * gain
    half = 0.5 * scaled
    return half + half * jnp.tanh(half)


def kernel(tms, nrows, lat_hbm, gain_ref, tw_hbm, tb_ref, sw_hbm, sb_ref, out_ref,
           tile, edge, halo, act, hact, tw, sw, folded, padded, wide, spread, woven,
           load_sem, send_sem, recv_sem):
    frames, height, width, chans = lat_hbm.shape
    couts = sb_ref.shape[1]
    tm = lax.axis_index("tm")
    row = lax.axis_index("rows")
    col = lax.axis_index("cols")
    tall = height + 2

    load_tile = pltpu.make_async_copy(lat_hbm, tile.at[2:, 1 : height + 1], load_sem.at[0])
    load_sw = pltpu.make_async_copy(sw_hbm, sw, load_sem.at[1])
    load_tw = pltpu.make_async_copy(tw_hbm, tw, load_sem.at[2])
    load_tile.start()
    load_sw.start()
    load_tw.start()

    def goes(kind):
        dt, dr, _ = kind
        return (tm + dt < tms) & (row + dr >= 0) & (row + dr < nrows)

    def comes(kind):
        dt, dr, _ = kind
        return (tm - dt >= 0) & (row - dr >= 0) & (row - dr < nrows)

    def count(test):
        return sum(jnp.where(test(kind), 1, 0) for kind in KINDS)

    barrier = pltpu.get_barrier_semaphore()
    for kind in KINDS:
        dt, dr, dc = kind

        @pl.when(comes(kind))
        def _():
            pl.semaphore_signal(
                barrier, inc=1, device_id_type=MESH,
                device_id={"tm": tm - dt, "rows": row - dr, "cols": 1 - col if dc else col})

    def copy_of(index):
        dt, dr, dc = KINDS[index]
        first = frames if dt else 2
        into = 0 if dt else 2
        size = 2 if dt else frames
        source_row, dest_row, rows = {0: (1, 1, height), 1: (height, 0, 1), -1: (1, height + 1, 1)}[dr]
        if dc:
            source = edge.at[pl.ds(first - 2, size), pl.ds(source_row - 1, rows)]
            dest = halo.at[pl.ds(into, size), pl.ds(dest_row, rows)]
        else:
            source = tile.at[pl.ds(first, size), pl.ds(source_row, rows)]
            dest = tile.at[pl.ds(into, size), pl.ds(dest_row, rows)]
        return pltpu.make_async_remote_copy(
            src_ref=source, dst_ref=dest, send_sem=send_sem.at[index], recv_sem=recv_sem.at[index],
            device_id={"tm": tm + dt, "rows": row + dr, "cols": 1 - col if dc else col}, device_id_type=MESH)

    @pl.when(tm == 0)
    def _():
        tile[0:2] = jnp.zeros_like(tile[0:2])
        halo[0:2] = jnp.zeros_like(halo[0:2])

    @pl.when(row == 0)
    def _():
        tile[:, 0:1] = jnp.zeros_like(tile[:, 0:1])
        halo[:, 0:1] = jnp.zeros_like(halo[:, 0:1])

    @pl.when(row == nrows - 1)
    def _():
        tile[:, tall - 1 :] = jnp.zeros_like(tile[:, tall - 1 :])
        halo[:, tall - 1 :] = jnp.zeros_like(halo[:, tall - 1 :])

    load_tile.wait()
    for f in range(frames):
        for i in range(height):
            last = tile[2 + f, 1 + i, width - 16 :, :].astype(F32)[15:16]
            head = tile[2 + f, 1 + i, :16, :].astype(F32)[0:1]
            edge[f, i] = jnp.where(col == 0, last, head)

    pl.semaphore_wait(barrier, count(goes))
    for index, kind in enumerate(KINDS):

        @pl.when(goes(kind))
        def _():
            copy_of(index).start()

    load_sw.wait()
    for b in range(3):
        tap = [sw[a, b].astype(F32) for a in range(3)]
        for p in range(2):
            for r in range(2):
                total = (tap[0], tap[1] + tap[2], tap[0] + tap[1], tap[2])[2 * p + r]
                spread[pl.ds((b * 4 + p * 2 + r) * chans, chans), :] = total
    for p in range(2):
        for r in range(2):
            if folded.shape[-1] > couts:
                folded[p, r, :, :, couts:] = jnp.zeros_like(folded[p, r, :, :, couts:])
            cols_sum = [spread[pl.ds((b * 4 + p * 2 + r) * chans, chans), :] for b in range(3)]
            folded[p, r, 0, :chans, :couts] = cols_sum[0].astype(BF16)
            folded[p, r, 0, chans:, :couts] = (cols_sum[1] + cols_sum[2]).astype(BF16)
            folded[p, r, 1, :chans, :couts] = (cols_sum[0] + cols_sum[1]).astype(BF16)
            folded[p, r, 1, chans:, :couts] = cols_sum[2].astype(BF16)
    load_tw.wait()

    for index, kind in enumerate(KINDS):

        @pl.when(comes(kind))
        def _():
            copy_of(index).wait_recv()

    gain = gain_ref[...]
    for f in range(frames + 2):
        act[f] = activate(tile[f].reshape(tall * width, chans), gain).astype(BF16)
        for i in range(tall):
            hact[pl.ds(f * tall + i, 1), :] = halo[f, i]
    hact[...] = activate(hact[...], gain)

    bias = tb_ref[...]
    count_in = frames * tall
    main = act[...].reshape((frames + 2) * tall * width, chans)
    side = hact[...]
    summed = bias + jnp.zeros((count_in * width, 2 * chans), F32)
    sides = bias + jnp.zeros((count_in, 2 * chans), F32)
    for k in range(3):
        first = k * tall
        weight = tw[k]
        summed += jnp.dot(main[first * width : (first + count_in) * width], weight, preferred_element_type=F32)
        sides += jnp.dot(side[first : first + count_in].astype(BF16), weight, preferred_element_type=F32)
    summed = summed.reshape(count_in, width, 2 * chans)
    for t in range(frames):
        for i in range(tall):
            g = t * tall + i
            center = summed[g]
            rim = sides[g : g + 1]
            if i == 0:
                center = jnp.where(row == 0, 0.0, center)
                rim = jnp.where(row == 0, 0.0, rim)
            if i == tall - 1:
                center = jnp.where(row == nrows - 1, 0.0, center)
                rim = jnp.where(row == nrows - 1, 0.0, rim)
            padded[g, 8 : 8 + width, :] = center
            padded[g, 7:8, :] = jnp.where(col == 0, 0.0, rim)
            padded[g, 8 + width : 9 + width, :] = jnp.where(col == 0, rim, 0.0)
    for t in range(frames):
        for i in range(tall):
            g = t * tall + i
            for shift in range(3):
                moved = padded[g, 7 + shift : 7 + shift + width, :].astype(BF16)
                for s in range(2):
                    wide[2 * t + s, i, :, shift * chans : (shift + 1) * chans] = moved[:, s * chans : (s + 1) * chans]

    cells = 2 * frames * height * width
    for p in range(2):
        for q in range(2):
            total = jnp.zeros((cells, folded.shape[-1]), F32)
            for r in range(2):
                patch = wide[:, p + r : p + r + height, :, q * chans : (q + 2) * chans].reshape(cells, 2 * chans)
                total += jnp.dot(patch, folded[p, r, q], preferred_element_type=F32)
            total = total.reshape(2 * frames, height, width, folded.shape[-1])
            for f in range(2 * frames):
                for i in range(height):
                    base = (f * 2 * height + 2 * i + p) * 2 * width
                    for h in range(woven.shape[0]):
                        woven[h, pl.ds(base + q, width, stride=2), :] = total[f, i, :, h * 128 : (h + 1) * 128]
    for f in range(2 * frames):
        for i in range(2 * height):
            base = (f * 2 * height + i) * 2 * width
            for h in range(woven.shape[0]):
                lanes = slice(h * 128, min(h * 128 + 128, couts))
                size = lanes.stop - lanes.start
                line = woven[h, base : base + 2 * width, :size] + sb_ref[:, lanes]
                out_ref[f, i, :, lanes] = line.astype(BF16)

    for index, kind in enumerate(KINDS):

        @pl.when(goes(kind))
        def _():
            copy_of(index).wait_send()


def local(tms, nrows, latent, norm_gain, time_weight, time_bias, space_weight, space_bias):
    frames, height, width, chans = latent.shape
    couts = space_bias.shape[0]
    tall = height + 2
    groups = frames * tall
    vmem = pl.BlockSpec(memory_space=pltpu.VMEM)
    anywhere = pl.BlockSpec(memory_space=pl.ANY)
    halves = pl.cdiv(couts, 128)
    return pl.pallas_call(
        functools.partial(kernel, tms, nrows),
        name="upsample",
        out_shape=jax.ShapeDtypeStruct((2 * frames, 2 * height, 2 * width, couts), BF16),
        in_specs=[anywhere, vmem, anywhere, vmem, anywhere, vmem],
        out_specs=vmem,
        scratch_shapes=[
            pltpu.VMEM((frames + 2, tall, width, chans), BF16),
            pltpu.VMEM((frames, height, 1, chans), F32),
            pltpu.VMEM((frames + 2, tall, 1, chans), F32),
            pltpu.VMEM((frames + 2, tall * width, chans), BF16),
            pltpu.VMEM(((frames + 2) * tall, chans), F32),
            pltpu.VMEM(time_weight.shape, BF16),
            pltpu.VMEM(space_weight.shape, BF16),
            pltpu.VMEM((2, 2, 2, 2 * chans, halves * 128), BF16),
            pltpu.VMEM((groups, width + 16, 2 * chans), F32),
            pltpu.VMEM((2 * frames, tall, width, 3 * chans), BF16),
            pltpu.VMEM((12 * chans, couts), F32),
            pltpu.VMEM((halves, 8 * frames * height * width, 128), F32),
            pltpu.SemaphoreType.DMA((3,)),
            pltpu.SemaphoreType.DMA((len(KINDS),)),
            pltpu.SemaphoreType.DMA((len(KINDS),)),
        ],
        compiler_params=pltpu.CompilerParams(
            collective_id=0, has_side_effects=True, vmem_limit_bytes=56 * 2**20),
    )(latent, norm_gain[None], time_weight, time_bias[None], space_weight, space_bias[None])


def solution(mesh):
    in_specs = (P(("clips", "tm"), "rows", "cols", None), P(), P(), P(), P(), P())
    out_specs = P(("clips", "tm"), "rows", "cols", None)
    body = functools.partial(local, mesh.shape["tm"], mesh.shape["rows"])
    return jax.shard_map(body, mesh=mesh, in_specs=in_specs, out_specs=out_specs, check_vma=False)
```

```python
import functools

import jax
import jax.numpy as jnp
from jax import lax
from jax.experimental import pallas as pl
from jax.experimental.pallas import tpu as pltpu
from jax.sharding import PartitionSpec as P

F32 = jnp.float32
BF16 = jnp.bfloat16
MESH = pl.DeviceIdType.MESH
KINDS = [
    (frame, dr, dc)
    for frame in (1, None, 0)
    for dc in (0, 1)
    for dr in (0, -1, 1)
    if (frame, dr, dc) != (None, 0, 0)
]


def activate(raw, gain):
    values = raw.astype(F32)
    mean_square = jnp.mean(values * values, axis=-1, keepdims=True)
    scaled = values * lax.rsqrt(mean_square + 1e-06) * gain
    half = 0.5 * scaled
    return half + half * jnp.tanh(half)


def kernel(tms, nrows, lat_hbm, gain_ref, tw_hbm, tb_ref, sw_hbm, sb_ref, out_ref,
           tile, edge, halo, halo_rows, act, acc, tw, sw, folded, padded, wide, woven,
           load_sem, send_sem, recv_sem):
    frames, height, width, chans = lat_hbm.shape
    couts = sb_ref.shape[-1]
    wide_couts = folded.shape[3]
    tm = lax.axis_index("tm")
    row = lax.axis_index("rows")
    col = lax.axis_index("cols")
    tall = height + 2
    cells = tall * width

    load_tile = pltpu.make_async_copy(lat_hbm, tile.at[2:, 1 : height + 1], load_sem.at[0])
    load_sw = pltpu.make_async_copy(sw_hbm, sw, load_sem.at[1])
    load_tw = pltpu.make_async_copy(tw_hbm, tw, load_sem.at[2])
    load_tile.start()
    load_sw.start()
    load_tw.start()

    def goes(kind):
        frame, dr, _ = kind
        return (tm + (frame is not None) < tms) & (row + dr >= 0) & (row + dr < nrows)

    def comes(kind):
        frame, dr, _ = kind
        return (tm - (frame is not None) >= 0) & (row - dr >= 0) & (row - dr < nrows)

    def count(test):
        return sum(jnp.where(test(kind), 1, 0) for kind in KINDS if kind[0] != 0)

    barrier = pltpu.get_barrier_semaphore()
    for kind in KINDS:
        frame, dr, dc = kind
        if frame == 0:
            continue

        @pl.when(comes(kind))
        def _():
            pl.semaphore_signal(
                barrier, inc=1, device_id_type=MESH,
                device_id={"tm": tm - (frame is not None), "rows": row - dr, "cols": 1 - col if dc else col})

    def copy_of(index):
        frame, dr, dc = KINDS[index]
        first, into, size = (2, 2, frames) if frame is None else (frames + frame, frame, 1)
        source_row, dest_row, rows = {0: (1, 1, height), 1: (height, 0, 1), -1: (1, height + 1, 1)}[dr]
        if dc:
            source = edge.at[pl.ds(first - 2, size), pl.ds(source_row - 1, rows)]
            dest = halo.at[pl.ds(into, size), pl.ds(dest_row, rows)]
        else:
            source = tile.at[pl.ds(first, size), pl.ds(source_row, rows)]
            dest = tile.at[pl.ds(into, size), pl.ds(dest_row, rows)]
        return pltpu.make_async_remote_copy(
            src_ref=source, dst_ref=dest, send_sem=send_sem.at[index], recv_sem=recv_sem.at[index],
            device_id={"tm": tm + (frame is not None), "rows": row + dr, "cols": 1 - col if dc else col},
            device_id_type=MESH)

    @pl.when(tm == 0)
    def _():
        tile[0:2] = jnp.zeros_like(tile[0:2])
        halo[0:2] = jnp.zeros_like(halo[0:2])

    @pl.when(row == 0)
    def _():
        tile[:, 0:1] = jnp.zeros_like(tile[:, 0:1])
        halo[:, 0:1] = jnp.zeros_like(halo[:, 0:1])

    @pl.when(row == nrows - 1)
    def _():
        tile[:, tall - 1 :] = jnp.zeros_like(tile[:, tall - 1 :])
        halo[:, tall - 1 :] = jnp.zeros_like(halo[:, tall - 1 :])

    load_tile.wait()
    for f in range(frames):
        for i in range(height):
            last = tile[2 + f, 1 + i, width - 16 :, :].astype(F32)[15:16]
            head = tile[2 + f, 1 + i, :16, :].astype(F32)[0:1]
            edge[f, i] = jnp.where(col == 0, last, head)

    pl.semaphore_wait(barrier, count(goes))
    for index, kind in enumerate(KINDS):

        @pl.when(goes(kind))
        def _():
            copy_of(index).start()

    gain = gain_ref[...].reshape(1, chans)
    halo_rows[...] = jnp.zeros_like(halo_rows)

    def activate_frame(f, begin, end):
        cut = tile[f, begin:end].reshape((end - begin) * width, chans)
        act[begin * width : end * width, f * chans : (f + 1) * chans] = activate(cut, gain).astype(BF16)

    def activate_halo(f):
        for i in range(tall):
            halo_rows[f, i : i + 1, :] = halo[f, i]
        act[cells:, f * chans : (f + 1) * chans] = activate(halo_rows[f], gain).astype(BF16)

    for f in range(frames):
        activate_frame(2 + f, 1, 1 + height)

    if wide_couts > couts:
        for p in range(2):
            for r in range(2):
                for q in range(2):
                    folded[p, r, q, couts:, :] = jnp.zeros((wide_couts - couts, 2 * chans), BF16)
    load_sw.wait()

    def fold(n, carry):
        span = pl.ds(pl.multiple_of(n * 16, 16), 16)
        sums = []
        for b in range(3):
            tap = [sw[a, b, span, :].astype(F32) for a in range(3)]
            sums.append((tap[0], tap[1] + tap[2], tap[0] + tap[1], tap[2]))
        for p in range(2):
            for r in range(2):
                left, middle, right = (sums[b][2 * p + r] for b in range(3))
                folded[p, r, 0, span, :chans] = left.astype(BF16)
                folded[p, r, 0, span, chans:] = (middle + right).astype(BF16)
                folded[p, r, 1, span, :chans] = (left + middle).astype(BF16)
                folded[p, r, 1, span, chans:] = right.astype(BF16)
        return carry

    lax.fori_loop(0, couts // 16, fold, 0)
    load_tw.wait()

    def await_frames(which):
        for index, kind in enumerate(KINDS):
            if kind[0] == which:

                @pl.when(comes(kind))
                def _():
                    copy_of(index).wait_recv()

    def taps(t, begin, end):
        size = (end - begin) * chans
        left = act[:, (t + begin) * chans : (t + end) * chans]
        return jnp.dot(left, tw[begin:end].reshape(size, 2 * chans), preferred_element_type=F32)

    await_frames(None)
    for f in range(frames):
        activate_frame(2 + f, 0, 1)
        activate_frame(2 + f, tall - 1, tall)
        activate_halo(2 + f)
    bias = tb_ref[...].reshape(1, 2 * chans)
    for t in range(frames):
        acc[t] = taps(t, max(2 - t, 0), 3) + bias

    await_frames(1)
    activate_frame(1, 0, tall)
    activate_halo(1)
    stores = []
    for t in reversed(range(frames)):
        if t == 0:
            await_frames(0)
            activate_frame(0, 0, tall)
            activate_halo(0)
        summed = acc[t]
        if t < 2:
            summed += taps(t, 0, 2 - t)
        for i in range(tall):
            center = summed[i * width : (i + 1) * width]
            rim = summed[cells + i : cells + i + 1]
            if i == 0:
                center = jnp.where(row == 0, 0.0, center)
                rim = jnp.where(row == 0, 0.0, rim)
            if i == tall - 1:
                center = jnp.where(row == nrows - 1, 0.0, center)
                rim = jnp.where(row == nrows - 1, 0.0, rim)
            padded[t, i, 8 : 8 + width, :] = center
            padded[t, i, 7:8, :] = jnp.where(col == 0, 0.0, rim)
            padded[t, i, 8 + width : 9 + width, :] = jnp.where(col == 0, rim, 0.0)
            for shift in range(3):
                moved = padded[t, i, 7 + shift : 7 + shift + width, :].astype(BF16)
                for s in range(2):
                    wide[2 * t + s, i, :, shift * chans : (shift + 1) * chans] = moved[:, s * chans : (s + 1) * chans]
        for p in range(2):
            for q in range(2):
                total = jnp.zeros((2 * height * width, wide_couts), F32)
                for r in range(2):
                    patch = wide[2 * t : 2 * t + 2, p + r : p + r + height, :, q * chans : (q + 2) * chans]
                    total += lax.dot_general(
                        patch.reshape(2 * height * width, 2 * chans), folded[p, r, q],
                        (((1,), (1,)), ((), ())), preferred_element_type=F32)
                for s in range(2):
                    for i in range(height):
                        base = ((2 * t + s) * 2 * height + 2 * i + p) * 2 * width
                        part = total[(s * height + i) * width : (s * height + i + 1) * width]
                        for h in range(woven.shape[0]):
                            woven[h, pl.ds(base + q, width, stride=2), :] = part[:, h * 128 : (h + 1) * 128]
        out_bias = sb_ref[...].reshape(1, couts)
        for f in range(2 * t, 2 * t + 2):
            for i in range(2 * height):
                base = (f * 2 * height + i) * 2 * width
                for h in range(woven.shape[0]):
                    lanes = slice(h * 128, min(h * 128 + 128, couts))
                    size = lanes.stop - lanes.start
                    line = woven[h, base : base + 2 * width, :size] + out_bias[:, lanes]
                    out_ref[f, i, :, lanes] = line.astype(BF16)

    for index, kind in enumerate(KINDS):

        @pl.when(goes(kind))
        def _():
            copy_of(index).wait_send()


def local(tms, nrows, latent, norm_gain, time_weight, time_bias, space_weight, space_bias):
    frames, height, width, chans = latent.shape
    couts = space_bias.shape[0]
    tall = height + 2
    spare = 16 * pl.cdiv(tall, 16)
    halves = pl.cdiv(couts, 128)
    vmem = pl.BlockSpec(memory_space=pltpu.VMEM)
    anywhere = pl.BlockSpec(memory_space=pltpu.HBM)
    return pl.pallas_call(
        functools.partial(kernel, tms, nrows),
        name="upsample",
        out_shape=pltpu.VMEM((2 * frames, 2 * height, 2 * width, couts), BF16),
        in_specs=[anywhere, vmem, anywhere, vmem, anywhere, vmem],
        out_specs=vmem,
        scratch_shapes=[
            pltpu.VMEM((frames + 2, tall, width, chans), BF16),
            pltpu.VMEM((frames, height, 1, chans), F32),
            pltpu.VMEM((frames + 2, tall, 1, chans), F32),
            pltpu.VMEM((frames + 2, spare, chans), F32),
            pltpu.VMEM((tall * width + spare, (frames + 2) * chans), BF16),
            pltpu.VMEM((frames, tall * width + spare, 2 * chans), F32),
            pltpu.VMEM(time_weight.shape, BF16),
            pltpu.VMEM((3, 3, couts, chans), BF16),
            pltpu.VMEM((2, 2, 2, halves * 128, 2 * chans), BF16),
            pltpu.VMEM((frames, tall, width + 16, 2 * chans), F32),
            pltpu.VMEM((2 * frames, tall, width, 3 * chans), BF16),
            pltpu.VMEM((halves, 8 * frames * height * width, 128), F32),
            pltpu.SemaphoreType.DMA((3,)),
            pltpu.SemaphoreType.DMA((len(KINDS),)),
            pltpu.SemaphoreType.DMA((len(KINDS),)),
        ],
        compiler_params=pltpu.CompilerParams(
            collective_id=0, has_side_effects=True, vmem_limit_bytes=56 * 2**20),
    )(latent, norm_gain, time_weight, time_bias, jnp.swapaxes(space_weight, 2, 3), space_bias)


def solution(mesh):
    in_specs = (P(("clips", "tm"), "rows", "cols", None), P(), P(), P(), P(), P())
    out_specs = P(("clips", "tm"), "rows", "cols", None)
    body = functools.partial(local, mesh.shape["tm"], mesh.shape["rows"])
    return jax.shard_map(body, mesh=mesh, in_specs=in_specs, out_specs=out_specs, check_vma=False)
```

```python
import functools

import jax
import jax.numpy as jnp
from jax import lax
from jax.experimental import pallas as pl
from jax.experimental.pallas import tpu as pltpu
from jax.sharding import PartitionSpec as P

F32 = jnp.float32
BF16 = jnp.bfloat16
MESH = pl.DeviceIdType.MESH
KINDS = [(0, dr, 0) for dr in (-1, 1)] + [(1, dr, 0) for dr in (0, -1, 1)]
EDGES = [(dt, dr, 1) for dt in (0, 1) for dr in (0, -1, 1)]
ALL = KINDS + EDGES
GROUPS = [(0, 0), (0, -1), (0, 1), (1, 0), (1, -1), (1, 1)]


def activate(raw, gain):
    values = raw.astype(F32)
    mean_square = jnp.mean(values * values, axis=-1, keepdims=True)
    scaled = values * lax.rsqrt(mean_square + 1e-06) * gain
    half = 0.5 * scaled
    return half + half * jnp.tanh(half)


def kernel(tms, nrows, lat_hbm, gain_ref, tw_hbm, tb_ref, sw_hbm, sb_ref, out_ref,
           tile, edge, halo, halo_rows, act, tw, sw, folded, padded, wide, woven,
           load_sem, send_sem, recv_sem):
    frames, height, width, chans = lat_hbm.shape
    couts = sb_ref.shape[-1]
    wide_couts = folded.shape[3]
    tm = lax.axis_index("tm")
    row = lax.axis_index("rows")
    col = lax.axis_index("cols")
    tall = height + 2
    cells = tall * width

    def when(ok, body):
        if ok is None:
            body()
        else:
            pl.when(ok)(body)

    def goes(dt, dr):
        tests = ([tm < tms - 1] if dt else []) + {0: [], -1: [row > 0], 1: [row < nrows - 1]}[dr]
        return functools.reduce(jnp.logical_and, tests) if tests else None

    def comes(dt, dr):
        tests = ([tm > 0] if dt else []) + {0: [], 1: [row > 0], -1: [row < nrows - 1]}[dr]
        return functools.reduce(jnp.logical_and, tests) if tests else None

    barrier = pltpu.get_barrier_semaphore()
    for dt, dr in GROUPS:

        def signal():
            for dc in (0, 1):
                if (dt, dr, dc) != (0, 0, 0):
                    pl.semaphore_signal(
                        barrier, inc=1, device_id_type=MESH,
                        device_id={"tm": tm - dt, "rows": row - dr, "cols": 1 - col if dc else col})

        when(comes(dt, dr), signal)

    load_tile = pltpu.make_async_copy(lat_hbm, tile.at[2:, 1 : height + 1], load_sem.at[0])
    load_sw = pltpu.make_async_copy(sw_hbm, sw, load_sem.at[1])
    load_tw = pltpu.make_async_copy(tw_hbm, tw, load_sem.at[2])
    load_tile.start()
    load_sw.start()
    load_tw.start()

    def copy_of(kind):
        dt, dr, dc = kind
        first, into, size = (frames - 2, 0, 2) if dt else (0, 2, frames)
        source_row, dest_row, rows = {0: (0, 1, height), 1: (height - 1, 0, 1), -1: (0, height + 1, 1)}[dr]
        source, dest = (edge, halo) if dc else (lat_hbm, tile)
        index = ALL.index(kind)
        return pltpu.make_async_remote_copy(
            src_ref=source.at[pl.ds(first, size), pl.ds(source_row, rows)],
            dst_ref=dest.at[pl.ds(into, size), pl.ds(dest_row, rows)],
            send_sem=send_sem.at[index], recv_sem=recv_sem.at[index],
            device_id={"tm": tm + dt, "rows": row + dr, "cols": 1 - col if dc else col}, device_id_type=MESH)

    vertical = jnp.where(row > 0, 1, 0) + jnp.where(row < nrows - 1, 1, 0)
    pl.semaphore_wait(barrier, 1 + 2 * vertical + jnp.where(tm < tms - 1, 2 + 2 * vertical, 0))
    for kind in KINDS:
        when(goes(*kind[:2]), lambda: copy_of(kind).start())

    load_tile.wait()
    for f in range(frames):
        for i in range(height):
            last = tile[2 + f, 1 + i, width - 16 :, :].astype(F32)[15:16]
            head = tile[2 + f, 1 + i, :16, :].astype(F32)[0:1]
            edge[f, i] = jnp.where(col == 0, last, head)
    for kind in EDGES:
        when(goes(*kind[:2]), lambda: copy_of(kind).start())

    @pl.when(tm == 0)
    def _():
        tile[0:2] = jnp.zeros_like(tile[0:2])
        halo[0:2] = jnp.zeros_like(halo[0:2])

    @pl.when(row == 0)
    def _():
        tile[:, 0:1] = jnp.zeros_like(tile[:, 0:1])
        halo[:, 0:1] = jnp.zeros_like(halo[:, 0:1])

    @pl.when(row == nrows - 1)
    def _():
        tile[:, tall - 1 :] = jnp.zeros_like(tile[:, tall - 1 :])
        halo[:, tall - 1 :] = jnp.zeros_like(halo[:, tall - 1 :])

    gain = gain_ref[...].reshape(1, chans)
    halo_rows[...] = jnp.zeros_like(halo_rows)

    def keep(f, begin, values):
        for k in range(3):
            if 0 <= f - k < frames:
                act[f - k, begin : begin + values.shape[0], k * chans : (k + 1) * chans] = values

    def activate_frame(f, begin, end):
        cut = tile[f, begin:end].reshape((end - begin) * width, chans)
        keep(f, begin * width, activate(cut, gain).astype(BF16))

    def activate_halo(f):
        for i in range(tall):
            halo_rows[f, i : i + 1, :] = halo[f, i]
        keep(f, cells, activate(halo_rows[f], gain).astype(BF16))

    for f in range(frames):
        activate_frame(2 + f, 1, 1 + height)

    if wide_couts > couts:
        for p in range(2):
            for r in range(2):
                for q in range(2):
                    folded[p, r, q, couts:, :] = jnp.zeros((wide_couts - couts, 2 * chans), BF16)
    load_sw.wait()

    def fold(n, carry):
        span = pl.ds(pl.multiple_of(n * 16, 16), 16)
        sums = []
        for b in range(3):
            tap = [sw[a, b, span, :].astype(F32) for a in range(3)]
            sums.append((tap[0], tap[1] + tap[2], tap[0] + tap[1], tap[2]))
        for p in range(2):
            for r in range(2):
                left, middle, right = (sums[b][2 * p + r] for b in range(3))
                folded[p, r, 0, span, :chans] = left.astype(BF16)
                folded[p, r, 0, span, chans:] = (middle + right).astype(BF16)
                folded[p, r, 1, span, :chans] = (left + middle).astype(BF16)
                folded[p, r, 1, span, chans:] = right.astype(BF16)
        return carry

    lax.fori_loop(0, couts // 16, fold, 0)
    load_tw.wait()

    for dt, dr in GROUPS:

        def receive():
            for dc in (0, 1):
                if (dt, dr, dc) != (0, 0, 0):
                    copy_of((dt, dr, dc)).wait_recv()

        when(comes(dt, dr), receive)

    for f in range(frames + 2):
        if f < 2:
            activate_frame(f, 0, tall)
        else:
            activate_frame(f, 0, 1)
            activate_frame(f, tall - 1, tall)
        activate_halo(f)

    span = act.shape[1]
    summed = jnp.dot(
        act[...].reshape(frames * span, 3 * chans), tw[...].reshape(3 * chans, 2 * chans), preferred_element_type=F32)
    summed += tb_ref[...].reshape(1, 2 * chans)
    for t in range(frames):
        for i in range(tall):
            center = summed[t * span + i * width : t * span + (i + 1) * width]
            rim = summed[t * span + cells + i : t * span + cells + i + 1]
            if i == 0:
                center = jnp.where(row == 0, 0.0, center)
                rim = jnp.where(row == 0, 0.0, rim)
            if i == tall - 1:
                center = jnp.where(row == nrows - 1, 0.0, center)
                rim = jnp.where(row == nrows - 1, 0.0, rim)
            padded[t, i, 8 : 8 + width, :] = center
            padded[t, i, 7:8, :] = jnp.where(col == 0, 0.0, rim)
            padded[t, i, 8 + width : 9 + width, :] = jnp.where(col == 0, rim, 0.0)
            for shift in range(3):
                moved = center if shift == 1 else padded[t, i, 7 + shift : 7 + shift + width, :]
                moved = moved.astype(BF16)
                for s in range(2):
                    wide[2 * t + s, i, :, shift * chans : (shift + 1) * chans] = moved[:, s * chans : (s + 1) * chans]

    size = 2 * frames * height * width
    out_bias = sb_ref[...].reshape(1, couts)
    for p in range(2):
        for q in range(2):
            total = jnp.zeros((size, wide_couts), F32)
            for r in range(2):
                patch = wide[:, p + r : p + r + height, :, q * chans : (q + 2) * chans]
                total += lax.dot_general(
                    patch.reshape(size, 2 * chans), folded[p, r, q],
                    (((1,), (1,)), ((), ())), preferred_element_type=F32)
            for f in range(2 * frames):
                for i in range(height):
                    base = (f * 2 * height + 2 * i + p) * 2 * width
                    part = total[(f * height + i) * width : (f * height + i + 1) * width]
                    for h in range(woven.shape[0]):
                        woven[h, pl.ds(base + q, width, stride=2), :] = part[:, h * 128 : (h + 1) * 128]
        for f in range(2 * frames):
            for i in range(p, 2 * height, 2):
                base = (f * 2 * height + i) * 2 * width
                for h in range(woven.shape[0]):
                    lanes = slice(h * 128, min(h * 128 + 128, couts))
                    line = woven[h, base : base + 2 * width, : lanes.stop - lanes.start] + out_bias[:, lanes]
                    out_ref[f, i, :, lanes] = line.astype(BF16)

    for dt, dr in GROUPS:

        def sent():
            for dc in (0, 1):
                if (dt, dr, dc) != (0, 0, 0):
                    copy_of((dt, dr, dc)).wait_send()

        when(goes(dt, dr), sent)


def local(tms, nrows, latent, norm_gain, time_weight, time_bias, space_weight, space_bias):
    frames, height, width, chans = latent.shape
    couts = space_bias.shape[0]
    tall = height + 2
    spare = 16 * pl.cdiv(tall, 16)
    halves = pl.cdiv(couts, 128)
    vmem = pl.BlockSpec(memory_space=pltpu.VMEM)
    anywhere = pl.BlockSpec(memory_space=pltpu.HBM)
    return pl.pallas_call(
        functools.partial(kernel, tms, nrows),
        name="upsample",
        out_shape=pltpu.VMEM((2 * frames, 2 * height, 2 * width, couts), BF16),
        in_specs=[anywhere, vmem, anywhere, vmem, anywhere, vmem],
        out_specs=vmem,
        scratch_shapes=[
            pltpu.VMEM((frames + 2, tall, width, chans), BF16),
            pltpu.VMEM((frames, height, 1, chans), F32),
            pltpu.VMEM((frames + 2, tall, 1, chans), F32),
            pltpu.VMEM((frames + 2, spare, chans), F32),
            pltpu.VMEM((frames, tall * width + spare, 3 * chans), BF16),
            pltpu.VMEM(time_weight.shape, BF16),
            pltpu.VMEM((3, 3, couts, chans), BF16),
            pltpu.VMEM((2, 2, 2, halves * 128, 2 * chans), BF16),
            pltpu.VMEM((frames, tall, width + 16, 2 * chans), F32),
            pltpu.VMEM((2 * frames, tall, width, 3 * chans), BF16),
            pltpu.VMEM((halves, 8 * frames * height * width, 128), F32),
            pltpu.SemaphoreType.DMA((3,)),
            pltpu.SemaphoreType.DMA((len(ALL),)),
            pltpu.SemaphoreType.DMA((len(ALL),)),
        ],
        compiler_params=pltpu.CompilerParams(
            collective_id=0, has_side_effects=True, vmem_limit_bytes=56 * 2**20),
    )(latent, norm_gain, time_weight, time_bias, jnp.swapaxes(space_weight, 2, 3), space_bias)


def solution(mesh):
    in_specs = (P(("clips", "tm"), "rows", "cols", None), P(), P(), P(), P(), P())
    out_specs = P(("clips", "tm"), "rows", "cols", None)
    body = functools.partial(local, mesh.shape["tm"], mesh.shape["rows"])
    return jax.shard_map(body, mesh=mesh, in_specs=in_specs, out_specs=out_specs, check_vma=False)
```

```python
import functools

import jax
import jax.numpy as jnp
from jax import lax
from jax.experimental import pallas as pl
from jax.experimental.pallas import tpu as pltpu
from jax.sharding import PartitionSpec as P

F32 = jnp.float32
BF16 = jnp.bfloat16
MESH = pl.DeviceIdType.MESH
KINDS = [(1, 0, 0), (0, -1, 0), (0, 1, 0), (1, -1, 0), (1, 1, 0)]
EDGES = [(dt, dr, 1) for dt in (0, 1) for dr in (0, -1, 1)]
ALL = KINDS + EDGES
GROUPS = [(0, 0), (0, -1), (0, 1), (1, 0), (1, -1), (1, 1)]


def activate(raw, gain):
    values = raw.astype(F32)
    mean_square = jnp.mean(values * values, axis=-1, keepdims=True)
    scaled = values * lax.rsqrt(mean_square + 1e-06) * gain
    half = 0.5 * scaled
    return half + half * jnp.tanh(half)


def kernel(tms, nrows, lat_hbm, gain_ref, tw_hbm, tb_ref, sw_hbm, sb_ref, out_ref,
           tile, edge, halo, halo_rows, act, acc, tw, sw, folded, padded, wide, woven,
           load_sem, send_sem, recv_sem):
    frames, height, width, chans = lat_hbm.shape
    couts = sb_ref.shape[-1]
    wide_couts = folded.shape[3]
    tm = lax.axis_index("tm")
    row = lax.axis_index("rows")
    col = lax.axis_index("cols")
    tall = height + 2
    cells = tall * width

    def when(ok, body):
        if ok is None:
            body()
        else:
            pl.when(ok)(body)

    def goes(dt, dr):
        tests = ([tm < tms - 1] if dt else []) + {0: [], -1: [row > 0], 1: [row < nrows - 1]}[dr]
        return functools.reduce(jnp.logical_and, tests) if tests else None

    def comes(dt, dr):
        tests = ([tm > 0] if dt else []) + {0: [], 1: [row > 0], -1: [row < nrows - 1]}[dr]
        return functools.reduce(jnp.logical_and, tests) if tests else None

    barrier = pltpu.get_barrier_semaphore()
    for dt, dr in GROUPS:

        def signal():
            for dc in (0, 1):
                if (dt, dr, dc) != (0, 0, 0):
                    pl.semaphore_signal(
                        barrier, inc=1, device_id_type=MESH,
                        device_id={"tm": tm - dt, "rows": row - dr, "cols": 1 - col if dc else col})

        when(comes(dt, dr), signal)

    load_tile = pltpu.make_async_copy(lat_hbm, tile.at[2:, 1 : height + 1], load_sem.at[0])
    load_sw = pltpu.make_async_copy(sw_hbm, sw, load_sem.at[1])
    load_tw = pltpu.make_async_copy(tw_hbm, tw, load_sem.at[2])
    load_tile.start()
    load_sw.start()
    load_tw.start()

    def copy_of(kind):
        dt, dr, dc = kind
        first, into, size = (frames - 2, 0, 2) if dt else (0, 2, frames)
        source_row, dest_row, rows = {0: (0, 1, height), 1: (height - 1, 0, 1), -1: (0, height + 1, 1)}[dr]
        source, dest = (edge, halo) if dc else (lat_hbm, tile)
        index = ALL.index(kind)
        return pltpu.make_async_remote_copy(
            src_ref=source.at[pl.ds(first, size), pl.ds(source_row, rows)],
            dst_ref=dest.at[pl.ds(into, size), pl.ds(dest_row, rows)],
            send_sem=send_sem.at[index], recv_sem=recv_sem.at[index],
            device_id={"tm": tm + dt, "rows": row + dr, "cols": 1 - col if dc else col}, device_id_type=MESH)

    vertical = jnp.where(row > 0, 1, 0) + jnp.where(row < nrows - 1, 1, 0)
    pl.semaphore_wait(barrier, 1 + 2 * vertical + jnp.where(tm < tms - 1, 2 + 2 * vertical, 0))
    for kind in KINDS:
        when(goes(*kind[:2]), lambda: copy_of(kind).start())

    load_tile.wait()
    for f in range(frames):
        for i in range(height):
            last = tile[2 + f, 1 + i, width - 16 :, :].astype(F32)[15:16]
            head = tile[2 + f, 1 + i, :16, :].astype(F32)[0:1]
            edge[f, i] = jnp.where(col == 0, last, head)
    for kind in EDGES:
        when(goes(*kind[:2]), lambda: copy_of(kind).start())

    @pl.when(tm == 0)
    def _():
        tile[0:2] = jnp.zeros_like(tile[0:2])
        halo[0:2] = jnp.zeros_like(halo[0:2])

    @pl.when(row == 0)
    def _():
        tile[:, 0:1] = jnp.zeros_like(tile[:, 0:1])
        halo[:, 0:1] = jnp.zeros_like(halo[:, 0:1])

    @pl.when(row == nrows - 1)
    def _():
        tile[:, tall - 1 :] = jnp.zeros_like(tile[:, tall - 1 :])
        halo[:, tall - 1 :] = jnp.zeros_like(halo[:, tall - 1 :])

    gain = gain_ref[...].reshape(1, chans)
    halo_rows[...] = jnp.zeros_like(halo_rows)

    def keep(f, begin, values):
        for k in range(3):
            if 0 <= f - k < frames:
                act[f - k, begin : begin + values.shape[0], k * chans : (k + 1) * chans] = values

    def activate_frame(f, begin, end):
        cut = tile[f, begin:end].reshape((end - begin) * width, chans)
        keep(f, begin * width, activate(cut, gain).astype(BF16))

    def activate_halo(f):
        for i in range(tall):
            halo_rows[f, i : i + 1, :] = halo[f, i]
        keep(f, cells, activate(halo_rows[f], gain).astype(BF16))

    for f in range(frames):
        activate_frame(2 + f, 1, 1 + height)

    if wide_couts > couts:
        for p in range(2):
            for r in range(2):
                for q in range(2):
                    folded[p, r, q, couts:, :] = jnp.zeros((wide_couts - couts, 2 * chans), BF16)
    load_sw.wait()

    def fold(n, carry):
        span = pl.ds(pl.multiple_of(n * 16, 16), 16)
        sums = []
        for b in range(3):
            tap = [sw[a, b, span, :].astype(F32) for a in range(3)]
            sums.append((tap[0], tap[1] + tap[2], tap[0] + tap[1], tap[2]))
        for p in range(2):
            for r in range(2):
                left, middle, right = (sums[b][2 * p + r] for b in range(3))
                folded[p, r, 0, span, :chans] = left.astype(BF16)
                folded[p, r, 0, span, chans:] = (middle + right).astype(BF16)
                folded[p, r, 1, span, :chans] = (left + middle).astype(BF16)
                folded[p, r, 1, span, chans:] = right.astype(BF16)
        return carry

    lax.fori_loop(0, couts // 16, fold, 0)
    load_tw.wait()

    def await_groups(step):
        for dt, dr in GROUPS:

            def receive():
                for dc in (0, 1):
                    if (dt, dr, dc) != (0, 0, 0):
                        copy_of((dt, dr, dc)).wait_recv()

            if dt == step:
                when(comes(dt, dr), receive)

    span = act.shape[1]

    def taps(begin, end):
        size = (end - begin) * chans
        return jnp.dot(
            act[:, :, begin * chans : end * chans].reshape(frames * span, size),
            tw[begin:end].reshape(size, 2 * chans), preferred_element_type=F32)

    await_groups(0)
    for f in range(2, frames + 2):
        activate_frame(f, 0, 1)
        activate_frame(f, tall - 1, tall)
        activate_halo(f)
    acc[...] = taps(2, 3) + tb_ref[...].reshape(1, 2 * chans)

    await_groups(1)
    for f in range(2):
        activate_frame(f, 0, tall)
        activate_halo(f)
    summed = acc[...] + taps(0, 2)
    for t in range(frames):
        for i in range(tall):
            center = summed[t * span + i * width : t * span + (i + 1) * width]
            rim = summed[t * span + cells + i : t * span + cells + i + 1]
            if i == 0:
                center = jnp.where(row == 0, 0.0, center)
                rim = jnp.where(row == 0, 0.0, rim)
            if i == tall - 1:
                center = jnp.where(row == nrows - 1, 0.0, center)
                rim = jnp.where(row == nrows - 1, 0.0, rim)
            padded[t, i, 8 : 8 + width, :] = center
            padded[t, i, 7:8, :] = jnp.where(col == 0, 0.0, rim)
            padded[t, i, 8 + width : 9 + width, :] = jnp.where(col == 0, rim, 0.0)
            for shift in range(3):
                moved = center if shift == 1 else padded[t, i, 7 + shift : 7 + shift + width, :]
                moved = moved.astype(BF16)
                for s in range(2):
                    wide[2 * t + s, i, :, shift * chans : (shift + 1) * chans] = moved[:, s * chans : (s + 1) * chans]

    size = 2 * frames * height * width
    out_bias = sb_ref[...].reshape(1, couts)
    for p in range(2):
        for q in range(2):
            total = jnp.zeros((size, wide_couts), F32)
            for r in range(2):
                patch = wide[:, p + r : p + r + height, :, q * chans : (q + 2) * chans]
                total += lax.dot_general(
                    patch.reshape(size, 2 * chans), folded[p, r, q],
                    (((1,), (1,)), ((), ())), preferred_element_type=F32)
            for f in range(2 * frames):
                for i in range(height):
                    base = (f * 2 * height + 2 * i + p) * 2 * width
                    part = total[(f * height + i) * width : (f * height + i + 1) * width]
                    for h in range(woven.shape[0]):
                        woven[h, pl.ds(base + q, width, stride=2), :] = part[:, h * 128 : (h + 1) * 128]
        for f in range(2 * frames):
            for i in range(p, 2 * height, 2):
                base = (f * 2 * height + i) * 2 * width
                for h in range(woven.shape[0]):
                    lanes = slice(h * 128, min(h * 128 + 128, couts))
                    line = woven[h, base : base + 2 * width, : lanes.stop - lanes.start] + out_bias[:, lanes]
                    out_ref[f, i, :, lanes] = line.astype(BF16)

    for dt, dr in GROUPS:

        def sent():
            for dc in (0, 1):
                if (dt, dr, dc) != (0, 0, 0):
                    copy_of((dt, dr, dc)).wait_send()

        when(goes(dt, dr), sent)


def local(tms, nrows, latent, norm_gain, time_weight, time_bias, space_weight, space_bias):
    frames, height, width, chans = latent.shape
    couts = space_bias.shape[0]
    tall = height + 2
    spare = 16 * pl.cdiv(tall, 16)
    halves = pl.cdiv(couts, 128)
    vmem = pl.BlockSpec(memory_space=pltpu.VMEM)
    anywhere = pl.BlockSpec(memory_space=pltpu.HBM)
    return pl.pallas_call(
        functools.partial(kernel, tms, nrows),
        name="upsample",
        out_shape=pltpu.VMEM((2 * frames, 2 * height, 2 * width, couts), BF16),
        in_specs=[anywhere, vmem, anywhere, vmem, anywhere, vmem],
        out_specs=vmem,
        scratch_shapes=[
            pltpu.VMEM((frames + 2, tall, width, chans), BF16),
            pltpu.VMEM((frames, height, 1, chans), F32),
            pltpu.VMEM((frames + 2, tall, 1, chans), F32),
            pltpu.VMEM((frames + 2, spare, chans), F32),
            pltpu.VMEM((frames, tall * width + spare, 3 * chans), BF16),
            pltpu.VMEM((frames * (tall * width + spare), 2 * chans), F32),
            pltpu.VMEM(time_weight.shape, BF16),
            pltpu.VMEM((3, 3, couts, chans), BF16),
            pltpu.VMEM((2, 2, 2, halves * 128, 2 * chans), BF16),
            pltpu.VMEM((frames, tall, width + 16, 2 * chans), F32),
            pltpu.VMEM((2 * frames, tall, width, 3 * chans), BF16),
            pltpu.VMEM((halves, 8 * frames * height * width, 128), F32),
            pltpu.SemaphoreType.DMA((3,)),
            pltpu.SemaphoreType.DMA((len(ALL),)),
            pltpu.SemaphoreType.DMA((len(ALL),)),
        ],
        compiler_params=pltpu.CompilerParams(
            collective_id=0, has_side_effects=True, vmem_limit_bytes=56 * 2**20),
    )(latent, norm_gain, time_weight, time_bias, jnp.swapaxes(space_weight, 2, 3), space_bias)


def solution(mesh):
    in_specs = (P(("clips", "tm"), "rows", "cols", None), P(), P(), P(), P(), P())
    out_specs = P(("clips", "tm"), "rows", "cols", None)
    body = functools.partial(local, mesh.shape["tm"], mesh.shape["rows"])
    return jax.shard_map(body, mesh=mesh, in_specs=in_specs, out_specs=out_specs, check_vma=False)
```

```python
import functools

import jax
import jax.numpy as jnp
from jax import lax
from jax.experimental import pallas as pl
from jax.experimental.pallas import tpu as pltpu
from jax.sharding import PartitionSpec as P

F32 = jnp.float32
BF16 = jnp.bfloat16
MESH = pl.DeviceIdType.MESH
KINDS = [(1, 0, 0), (0, -1, 0), (0, 1, 0), (1, -1, 0), (1, 1, 0)]
EDGES = [(dt, dr, 1) for dt in (0, 1) for dr in (0, -1, 1)]
ALL = KINDS + EDGES
GROUPS = [(0, 0), (0, -1), (0, 1), (1, 0), (1, -1), (1, 1)]


def activate(raw, gain):
    values = raw.astype(F32)
    mean_square = jnp.mean(values * values, axis=-1, keepdims=True)
    scaled = values * lax.rsqrt(mean_square + 1e-06) * gain
    half = 0.5 * scaled
    return half + half * jnp.tanh(half)


def kernel(tms, nrows, lat_hbm, gain_ref, tw_hbm, tb_ref, sw_hbm, sb_ref, out_ref,
           tile, edge, halo, halo_rows, act, acc, tw, sw, folded, padded, wide, woven,
           load_sem, send_sem, recv_sem):
    frames, height, width, chans = lat_hbm.shape
    couts = sb_ref.shape[-1]
    wide_couts = folded.shape[3]
    tm = lax.axis_index("tm")
    row = lax.axis_index("rows")
    col = lax.axis_index("cols")
    tall = height + 2
    cells = tall * width

    def when(ok, body):
        if ok is None:
            body()
        else:
            pl.when(ok)(body)

    def goes(dt, dr):
        tests = ([tm < tms - 1] if dt else []) + {0: [], -1: [row > 0], 1: [row < nrows - 1]}[dr]
        return functools.reduce(jnp.logical_and, tests) if tests else None

    def comes(dt, dr):
        tests = ([tm > 0] if dt else []) + {0: [], 1: [row > 0], -1: [row < nrows - 1]}[dr]
        return functools.reduce(jnp.logical_and, tests) if tests else None

    barrier = pltpu.get_barrier_semaphore()
    for dt, dr in GROUPS:

        def signal():
            for dc in (0, 1):
                if (dt, dr, dc) != (0, 0, 0):
                    pl.semaphore_signal(
                        barrier, inc=1, device_id_type=MESH,
                        device_id={"tm": tm - dt, "rows": row - dr, "cols": 1 - col if dc else col})

        when(comes(dt, dr), signal)

    load_tile = pltpu.make_async_copy(lat_hbm, tile.at[2:, 1 : height + 1], load_sem.at[0])
    load_sw = pltpu.make_async_copy(sw_hbm, sw, load_sem.at[1])
    load_tw = pltpu.make_async_copy(tw_hbm, tw, load_sem.at[2])
    load_tile.start()
    load_sw.start()
    load_tw.start()

    def copy_of(kind):
        dt, dr, dc = kind
        first, into, size = (frames - 2, 0, 2) if dt else (0, 2, frames)
        source_row, dest_row, rows = {0: (0, 1, height), 1: (height - 1, 0, 1), -1: (0, height + 1, 1)}[dr]
        source, dest = (edge, halo) if dc else (lat_hbm, tile)
        index = ALL.index(kind)
        return pltpu.make_async_remote_copy(
            src_ref=source.at[pl.ds(first, size), pl.ds(source_row, rows)],
            dst_ref=dest.at[pl.ds(into, size), pl.ds(dest_row, rows)],
            send_sem=send_sem.at[index], recv_sem=recv_sem.at[index],
            device_id={"tm": tm + dt, "rows": row + dr, "cols": 1 - col if dc else col}, device_id_type=MESH)

    vertical = jnp.where(row > 0, 1, 0) + jnp.where(row < nrows - 1, 1, 0)
    pl.semaphore_wait(barrier, 1 + 2 * vertical + jnp.where(tm < tms - 1, 2 + 2 * vertical, 0))
    for kind in KINDS:
        when(goes(*kind[:2]), lambda: copy_of(kind).start())

    load_tile.wait()
    for f in range(frames):
        for i in range(height):
            last = tile[2 + f, 1 + i, width - 16 :, :].astype(F32)[15:16]
            head = tile[2 + f, 1 + i, :16, :].astype(F32)[0:1]
            edge[f, i] = jnp.where(col == 0, last, head)
    for kind in EDGES:
        when(goes(*kind[:2]), lambda: copy_of(kind).start())

    @pl.when(tm == 0)
    def _():
        tile[0:2] = jnp.zeros_like(tile[0:2])
        halo[0:2] = jnp.zeros_like(halo[0:2])

    @pl.when(row == 0)
    def _():
        tile[:, 0:1] = jnp.zeros_like(tile[:, 0:1])
        halo[:, 0:1] = jnp.zeros_like(halo[:, 0:1])

    @pl.when(row == nrows - 1)
    def _():
        tile[:, tall - 1 :] = jnp.zeros_like(tile[:, tall - 1 :])
        halo[:, tall - 1 :] = jnp.zeros_like(halo[:, tall - 1 :])

    gain = gain_ref[...].reshape(1, chans)
    halo_rows[...] = jnp.zeros_like(halo_rows)

    def keep(f, begin, values):
        for k in range(3):
            if 0 <= f - k < frames:
                act[f - k, begin : begin + values.shape[0], k * chans : (k + 1) * chans] = values

    own = height * width

    def place(i):
        return own if i == 0 else own + width if i == tall - 1 else (i - 1) * width

    def activate_frame(f, begin, end):
        cut = tile[f, begin:end].reshape((end - begin) * width, chans)
        keep(f, place(begin), activate(cut, gain).astype(BF16))

    def activate_halo(f):
        for i in range(tall):
            halo_rows[f, i : i + 1, :] = halo[f, i]
        keep(f, cells, activate(halo_rows[f], gain).astype(BF16))

    for f in range(frames):
        activate_frame(2 + f, 1, 1 + height)

    if wide_couts > couts:
        for p in range(2):
            for r in range(2):
                for q in range(2):
                    folded[p, r, q, couts:, :] = jnp.zeros((wide_couts - couts, 2 * chans), BF16)
    load_sw.wait()

    def fold(n, carry):
        span = pl.ds(pl.multiple_of(n * 16, 16), 16)
        sums = []
        for b in range(3):
            tap = [sw[a, b, span, :].astype(F32) for a in range(3)]
            sums.append((tap[0], tap[1] + tap[2], tap[0] + tap[1], tap[2]))
        for p in range(2):
            for r in range(2):
                left, middle, right = (sums[b][2 * p + r] for b in range(3))
                folded[p, r, 0, span, :chans] = left.astype(BF16)
                folded[p, r, 0, span, chans:] = (middle + right).astype(BF16)
                folded[p, r, 1, span, :chans] = (left + middle).astype(BF16)
                folded[p, r, 1, span, chans:] = right.astype(BF16)
        return carry

    lax.fori_loop(0, couts // 16, fold, 0)
    load_tw.wait()

    def await_groups(groups):
        for dt, dr in groups:

            def receive():
                for dc in (0, 1):
                    if (dt, dr, dc) != (0, 0, 0):
                        copy_of((dt, dr, dc)).wait_recv()

            when(comes(dt, dr), receive)

    def taps(begin, end, low, high):
        depth = (end - begin) * chans
        product = jnp.dot(
            act[:, low:high, begin * chans : end * chans].reshape(frames * (high - low), depth),
            tw[begin:end].reshape(depth, 2 * chans), preferred_element_type=F32)
        return product.reshape(frames, high - low, 2 * chans)

    def put(t, i, shift, values):
        values = values.astype(BF16)
        for s in range(2):
            wide[2 * t + s, i, :, shift * chans : (shift + 1) * chans] = values[:, s * chans : (s + 1) * chans]

    def inside(i, values):
        if i == 0:
            return jnp.where(row == 0, 0.0, values)
        if i == tall - 1:
            return jnp.where(row == nrows - 1, 0.0, values)
        return values

    span = act.shape[1]
    await_groups([(0, 0), (0, -1), (0, 1)])
    for f in range(2, frames + 2):
        activate_frame(f, 0, 1)
        activate_frame(f, tall - 1, tall)
        activate_halo(f)
    acc[...] = taps(2, 3, 0, span) + tb_ref[...].reshape(1, 1, 2 * chans)

    await_groups([(1, 0)])
    for f in range(2):
        activate_frame(f, 1, 1 + height)
    summed = acc[:, :own] + taps(0, 2, 0, own)
    for t in range(frames):
        for i in range(1, 1 + height):
            center = summed[t, place(i) : place(i) + width]
            padded[t, i, 8 : 8 + width, :] = center
            put(t, i, 1, center)

    await_groups([(1, -1), (1, 1)])
    for f in range(2):
        activate_frame(f, 0, 1)
        activate_frame(f, tall - 1, tall)
        activate_halo(f)
    summed = acc[:, own:] + taps(0, 2, own, span)
    for t in range(frames):
        for i in range(tall):
            if i in (0, tall - 1):
                center = inside(i, summed[t, place(i) - own : place(i) - own + width])
                padded[t, i, 8 : 8 + width, :] = center
                put(t, i, 1, center)
            rim = inside(i, summed[t, 2 * width + i : 2 * width + i + 1])
            padded[t, i, 7:8, :] = jnp.where(col == 0, 0.0, rim)
            padded[t, i, 8 + width : 9 + width, :] = jnp.where(col == 0, rim, 0.0)
            for shift in (0, 2):
                put(t, i, shift, padded[t, i, 7 + shift : 7 + shift + width, :])

    size = 2 * frames * height * width
    out_bias = sb_ref[...].reshape(1, couts)
    for p in range(2):
        for q in range(2):
            total = jnp.zeros((size, wide_couts), F32)
            for r in range(2):
                patch = wide[:, p + r : p + r + height, :, q * chans : (q + 2) * chans]
                total += lax.dot_general(
                    patch.reshape(size, 2 * chans), folded[p, r, q],
                    (((1,), (1,)), ((), ())), preferred_element_type=F32)
            for f in range(2 * frames):
                for i in range(height):
                    base = (f * 2 * height + 2 * i + p) * 2 * width
                    part = total[(f * height + i) * width : (f * height + i + 1) * width]
                    for h in range(woven.shape[0]):
                        woven[h, pl.ds(base + q, width, stride=2), :] = part[:, h * 128 : (h + 1) * 128]
        for f in range(2 * frames):
            for i in range(p, 2 * height, 2):
                base = (f * 2 * height + i) * 2 * width
                for h in range(woven.shape[0]):
                    lanes = slice(h * 128, min(h * 128 + 128, couts))
                    line = woven[h, base : base + 2 * width, : lanes.stop - lanes.start] + out_bias[:, lanes]
                    out_ref[f, i, :, lanes] = line.astype(BF16)

    for dt, dr in GROUPS:

        def sent():
            for dc in (0, 1):
                if (dt, dr, dc) != (0, 0, 0):
                    copy_of((dt, dr, dc)).wait_send()

        when(goes(dt, dr), sent)


def local(tms, nrows, latent, norm_gain, time_weight, time_bias, space_weight, space_bias):
    frames, height, width, chans = latent.shape
    couts = space_bias.shape[0]
    tall = height + 2
    spare = 16 * pl.cdiv(tall, 16)
    halves = pl.cdiv(couts, 128)
    vmem = pl.BlockSpec(memory_space=pltpu.VMEM)
    anywhere = pl.BlockSpec(memory_space=pltpu.HBM)
    return pl.pallas_call(
        functools.partial(kernel, tms, nrows),
        name="upsample",
        out_shape=pltpu.VMEM((2 * frames, 2 * height, 2 * width, couts), BF16),
        in_specs=[anywhere, vmem, anywhere, vmem, anywhere, vmem],
        out_specs=vmem,
        scratch_shapes=[
            pltpu.VMEM((frames + 2, tall, width, chans), BF16),
            pltpu.VMEM((frames, height, 1, chans), F32),
            pltpu.VMEM((frames + 2, tall, 1, chans), F32),
            pltpu.VMEM((frames + 2, spare, chans), F32),
            pltpu.VMEM((frames, tall * width + spare, 3 * chans), BF16),
            pltpu.VMEM((frames, tall * width + spare, 2 * chans), F32),
            pltpu.VMEM(time_weight.shape, BF16),
            pltpu.VMEM((3, 3, couts, chans), BF16),
            pltpu.VMEM((2, 2, 2, halves * 128, 2 * chans), BF16),
            pltpu.VMEM((frames, tall, width + 16, 2 * chans), F32),
            pltpu.VMEM((2 * frames, tall, width, 3 * chans), BF16),
            pltpu.VMEM((halves, 8 * frames * height * width, 128), F32),
            pltpu.SemaphoreType.DMA((3,)),
            pltpu.SemaphoreType.DMA((len(ALL),)),
            pltpu.SemaphoreType.DMA((len(ALL),)),
        ],
        compiler_params=pltpu.CompilerParams(
            collective_id=0, has_side_effects=True, vmem_limit_bytes=56 * 2**20),
    )(latent, norm_gain, time_weight, time_bias, jnp.swapaxes(space_weight, 2, 3), space_bias)


def solution(mesh):
    in_specs = (P(("clips", "tm"), "rows", "cols", None), P(), P(), P(), P(), P())
    out_specs = P(("clips", "tm"), "rows", "cols", None)
    body = functools.partial(local, mesh.shape["tm"], mesh.shape["rows"])
    return jax.shard_map(body, mesh=mesh, in_specs=in_specs, out_specs=out_specs, check_vma=False)
```

```python
import functools

import jax
import jax.numpy as jnp
from jax import lax
from jax.experimental import pallas as pl
from jax.experimental.pallas import tpu as pltpu
from jax.sharding import PartitionSpec as P

F32 = jnp.float32
BF16 = jnp.bfloat16
MESH = pl.DeviceIdType.MESH
KINDS = [(1, 0, 0), (0, -1, 0), (0, 1, 0), (1, -1, 0), (1, 1, 0)]
EDGES = [(dt, dr, 1) for dt in (0, 1) for dr in (0, -1, 1)]
ALL = KINDS + EDGES
GROUPS = [(0, 0), (0, -1), (0, 1), (1, 0), (1, -1), (1, 1)]


def activate(raw, gain):
    values = raw.astype(F32)
    mean_square = jnp.mean(values * values, axis=-1, keepdims=True)
    scaled = values * lax.rsqrt(mean_square + 1e-06) * gain
    half = 0.5 * scaled
    return half + half * jnp.tanh(half)


def kernel(tms, nrows, lat_hbm, gain_ref, tw_hbm, tb_ref, sw_hbm, sb_ref, out_ref,
           tile, edge, halo, halo_rows, act, acc, tw, sw, folded, padded, wide, woven,
           load_sem, send_sem, recv_sem):
    frames, height, width, chans = lat_hbm.shape
    couts = sb_ref.shape[-1]
    wide_couts = folded.shape[3]
    tm = lax.axis_index("tm")
    row = lax.axis_index("rows")
    col = lax.axis_index("cols")
    tall = height + 2
    cells = tall * width

    def when(ok, body):
        if ok is None:
            body()
        else:
            pl.when(ok)(body)

    def goes(dt, dr):
        tests = ([tm < tms - 1] if dt else []) + {0: [], -1: [row > 0], 1: [row < nrows - 1]}[dr]
        return functools.reduce(jnp.logical_and, tests) if tests else None

    def comes(dt, dr):
        tests = ([tm > 0] if dt else []) + {0: [], 1: [row > 0], -1: [row < nrows - 1]}[dr]
        return functools.reduce(jnp.logical_and, tests) if tests else None

    barrier = pltpu.get_barrier_semaphore()
    for dt, dr in GROUPS:

        def signal():
            for dc in (0, 1):
                if (dt, dr, dc) != (0, 0, 0):
                    pl.semaphore_signal(
                        barrier, inc=1, device_id_type=MESH,
                        device_id={"tm": tm - dt, "rows": row - dr, "cols": 1 - col if dc else col})

        when(comes(dt, dr), signal)

    load_tile = pltpu.make_async_copy(lat_hbm, tile.at[2:, 1 : height + 1], load_sem.at[0])
    load_sw = pltpu.make_async_copy(sw_hbm, sw, load_sem.at[1])
    load_tw = pltpu.make_async_copy(tw_hbm, tw, load_sem.at[2])
    load_tile.start()
    load_sw.start()
    load_tw.start()

    def copy_of(kind):
        dt, dr, dc = kind
        first, into, size = (frames - 2, 0, 2) if dt else (0, 2, frames)
        source_row, dest_row, rows = {0: (0, 1, height), 1: (height - 1, 0, 1), -1: (0, height + 1, 1)}[dr]
        source, dest = (edge, halo) if dc else (lat_hbm, tile)
        index = ALL.index(kind)
        return pltpu.make_async_remote_copy(
            src_ref=source.at[pl.ds(first, size), pl.ds(source_row, rows)],
            dst_ref=dest.at[pl.ds(into, size), pl.ds(dest_row, rows)],
            send_sem=send_sem.at[index], recv_sem=recv_sem.at[index],
            device_id={"tm": tm + dt, "rows": row + dr, "cols": 1 - col if dc else col}, device_id_type=MESH)

    vertical = jnp.where(row > 0, 1, 0) + jnp.where(row < nrows - 1, 1, 0)
    pl.semaphore_wait(barrier, 1 + 2 * vertical + jnp.where(tm < tms - 1, 2 + 2 * vertical, 0))
    for kind in KINDS[:3]:
        when(goes(*kind[:2]), lambda: copy_of(kind).start())

    load_tile.wait()
    for f in range(frames):
        for i in range(height):
            last = tile[2 + f, 1 + i, width - 16 :, :].astype(F32)[15:16]
            head = tile[2 + f, 1 + i, :16, :].astype(F32)[0:1]
            edge[f, i] = jnp.where(col == 0, last, head)
    for kind in EDGES + KINDS[3:]:
        when(goes(*kind[:2]), lambda: copy_of(kind).start())

    @pl.when(tm == 0)
    def _():
        tile[0:2] = jnp.zeros_like(tile[0:2])
        halo[0:2] = jnp.zeros_like(halo[0:2])

    @pl.when(row == 0)
    def _():
        tile[:, 0:1] = jnp.zeros_like(tile[:, 0:1])
        halo[:, 0:1] = jnp.zeros_like(halo[:, 0:1])

    @pl.when(row == nrows - 1)
    def _():
        tile[:, tall - 1 :] = jnp.zeros_like(tile[:, tall - 1 :])
        halo[:, tall - 1 :] = jnp.zeros_like(halo[:, tall - 1 :])

    gain = gain_ref[...].reshape(1, chans)
    halo_rows[...] = jnp.zeros_like(halo_rows)

    def keep(f, begin, values):
        for k in range(3):
            if 0 <= f - k < frames:
                act[f - k, begin : begin + values.shape[0], k * chans : (k + 1) * chans] = values

    own = height * width

    def place(i):
        return own if i == 0 else own + width if i == tall - 1 else (i - 1) * width

    def activate_frame(f, begin, end):
        cut = tile[f, begin:end].reshape((end - begin) * width, chans)
        keep(f, place(begin), activate(cut, gain).astype(BF16))

    def activate_halo(f):
        for i in range(tall):
            halo_rows[f, i : i + 1, :] = halo[f, i]
        keep(f, cells, activate(halo_rows[f], gain).astype(BF16))

    for f in range(frames):
        activate_frame(2 + f, 1, 1 + height)

    if wide_couts > couts:
        for p in range(2):
            for r in range(2):
                for q in range(2):
                    folded[p, r, q, couts:, :] = jnp.zeros((wide_couts - couts, 2 * chans), BF16)
    load_sw.wait()

    def fold(n, carry):
        span = pl.ds(pl.multiple_of(n * 16, 16), 16)
        sums = []
        for b in range(3):
            tap = [sw[a, b, span, :].astype(F32) for a in range(3)]
            sums.append((tap[0], tap[1] + tap[2], tap[0] + tap[1], tap[2]))
        for p in range(2):
            for r in range(2):
                left, middle, right = (sums[b][2 * p + r] for b in range(3))
                folded[p, r, 0, span, :chans] = left.astype(BF16)
                folded[p, r, 0, span, chans:] = (middle + right).astype(BF16)
                folded[p, r, 1, span, :chans] = (left + middle).astype(BF16)
                folded[p, r, 1, span, chans:] = right.astype(BF16)
        return carry

    lax.fori_loop(0, couts // 16, fold, 0)
    load_tw.wait()

    def await_groups(groups):
        for dt, dr in groups:

            def receive():
                for dc in (0, 1):
                    if (dt, dr, dc) != (0, 0, 0):
                        copy_of((dt, dr, dc)).wait_recv()

            when(comes(dt, dr), receive)

    def taps(begin, end, low, high):
        depth = (end - begin) * chans
        product = jnp.dot(
            act[:, low:high, begin * chans : end * chans].reshape(frames * (high - low), depth),
            tw[begin:end].reshape(depth, 2 * chans), preferred_element_type=F32)
        return product.reshape(frames, high - low, 2 * chans)

    def put(t, i, shift, values):
        values = values.astype(BF16)
        for s in range(2):
            wide[2 * t + s, i, :, shift * chans : (shift + 1) * chans] = values[:, s * chans : (s + 1) * chans]

    def inside(i, values):
        if i == 0:
            return jnp.where(row == 0, 0.0, values)
        if i == tall - 1:
            return jnp.where(row == nrows - 1, 0.0, values)
        return values

    span = act.shape[1]
    await_groups([(0, 0), (0, -1), (0, 1)])
    for f in range(2, frames + 2):
        activate_frame(f, 0, 1)
        activate_frame(f, tall - 1, tall)
        activate_halo(f)
    acc[...] = taps(2, 3, 0, span) + tb_ref[...].reshape(1, 1, 2 * chans)

    await_groups([(1, 0)])
    for f in range(2):
        activate_frame(f, 1, 1 + height)
    summed = acc[:, :own] + taps(0, 2, 0, own)
    for t in range(frames):
        for i in range(1, 1 + height):
            center = summed[t, place(i) : place(i) + width]
            padded[t, i, 8 : 8 + width, :] = center
            put(t, i, 1, center)

    await_groups([(1, -1), (1, 1)])
    for f in range(2):
        activate_frame(f, 0, 1)
        activate_frame(f, tall - 1, tall)
        activate_halo(f)
    summed = acc[:, own:] + taps(0, 2, own, span)
    for t in range(frames):
        for i in range(tall):
            if i in (0, tall - 1):
                center = inside(i, summed[t, place(i) - own : place(i) - own + width])
                padded[t, i, 8 : 8 + width, :] = center
                put(t, i, 1, center)
            rim = inside(i, summed[t, 2 * width + i : 2 * width + i + 1])
            padded[t, i, 7:8, :] = jnp.where(col == 0, 0.0, rim)
            padded[t, i, 8 + width : 9 + width, :] = jnp.where(col == 0, rim, 0.0)
            for shift in (0, 2):
                put(t, i, shift, padded[t, i, 7 + shift : 7 + shift + width, :])

    size = 2 * frames * height * width
    out_bias = sb_ref[...].reshape(1, couts)
    for p in range(2):
        for q in range(2):
            total = jnp.zeros((size, wide_couts), F32)
            for r in range(2):
                patch = wide[:, p + r : p + r + height, :, q * chans : (q + 2) * chans]
                total += lax.dot_general(
                    patch.reshape(size, 2 * chans), folded[p, r, q],
                    (((1,), (1,)), ((), ())), preferred_element_type=F32)
            for f in range(2 * frames):
                for i in range(height):
                    base = (f * 2 * height + 2 * i + p) * 2 * width
                    part = total[(f * height + i) * width : (f * height + i + 1) * width]
                    for h in range(woven.shape[0]):
                        woven[h, pl.ds(base + q, width, stride=2), :] = part[:, h * 128 : (h + 1) * 128]
        for f in range(2 * frames):
            for i in range(p, 2 * height, 2):
                base = (f * 2 * height + i) * 2 * width
                for h in range(woven.shape[0]):
                    lanes = slice(h * 128, min(h * 128 + 128, couts))
                    line = woven[h, base : base + 2 * width, : lanes.stop - lanes.start] + out_bias[:, lanes]
                    out_ref[f, i, :, lanes] = line.astype(BF16)

    for dt, dr in GROUPS:

        def sent():
            for dc in (0, 1):
                if (dt, dr, dc) != (0, 0, 0):
                    copy_of((dt, dr, dc)).wait_send()

        when(goes(dt, dr), sent)


def local(tms, nrows, latent, norm_gain, time_weight, time_bias, space_weight, space_bias):
    frames, height, width, chans = latent.shape
    couts = space_bias.shape[0]
    tall = height + 2
    spare = 16 * pl.cdiv(tall, 16)
    halves = pl.cdiv(couts, 128)
    vmem = pl.BlockSpec(memory_space=pltpu.VMEM)
    anywhere = pl.BlockSpec(memory_space=pltpu.HBM)
    return pl.pallas_call(
        functools.partial(kernel, tms, nrows),
        name="upsample",
        out_shape=pltpu.VMEM((2 * frames, 2 * height, 2 * width, couts), BF16),
        in_specs=[anywhere, vmem, anywhere, vmem, anywhere, vmem],
        out_specs=vmem,
        scratch_shapes=[
            pltpu.VMEM((frames + 2, tall, width, chans), BF16),
            pltpu.VMEM((frames, height, 1, chans), F32),
            pltpu.VMEM((frames + 2, tall, 1, chans), F32),
            pltpu.VMEM((frames + 2, spare, chans), F32),
            pltpu.VMEM((frames, tall * width + spare, 3 * chans), BF16),
            pltpu.VMEM((frames, tall * width + spare, 2 * chans), F32),
            pltpu.VMEM(time_weight.shape, BF16),
            pltpu.VMEM((3, 3, couts, chans), BF16),
            pltpu.VMEM((2, 2, 2, halves * 128, 2 * chans), BF16),
            pltpu.VMEM((frames, tall, width + 16, 2 * chans), F32),
            pltpu.VMEM((2 * frames, tall, width, 3 * chans), BF16),
            pltpu.VMEM((halves, 8 * frames * height * width, 128), F32),
            pltpu.SemaphoreType.DMA((3,)),
            pltpu.SemaphoreType.DMA((len(ALL),)),
            pltpu.SemaphoreType.DMA((len(ALL),)),
        ],
        compiler_params=pltpu.CompilerParams(
            collective_id=0, has_side_effects=True, vmem_limit_bytes=56 * 2**20),
    )(latent, norm_gain, time_weight, time_bias, jnp.swapaxes(space_weight, 2, 3), space_bias)


def solution(mesh):
    in_specs = (P(("clips", "tm"), "rows", "cols", None), P(), P(), P(), P(), P())
    out_specs = P(("clips", "tm"), "rows", "cols", None)
    body = functools.partial(local, mesh.shape["tm"], mesh.shape["rows"])
    return jax.shard_map(body, mesh=mesh, in_specs=in_specs, out_specs=out_specs, check_vma=False)
```
